32 devices in a mesh: space: 8 (over z, x), vel: 4 (over y, core).
Axes of the slice: x: 2, y: 2, z: 4, core: 2. Of those that a mesh axis runs over, the one named last changes fastest.
Arguments:
- probe_field: float32 [2, 1024, 1024], P(None, 'space'), may hold values from -6 to 6
- control_field: float32 [2, 1024, 1024], P(None, 'space'), may hold values from -4 to 4
- optical_state: float32 [2, 64, 1024, 1024], P(None, 'vel', 'space'), may hold values from -3 to 3
- spin_state: float32 [2, 64, 1024, 1024], P(None, 'vel', 'space'), may hold values from -3 to 3
- doppler_shift: float32 [64], P('vel'), may hold values from -3 to 3
- class_weight: float32 [64], P('vel'), may hold values from 0.2 to 2
- gradient_shift: float32 [1024, 1024], P('space'), may hold values from -3 to 3
Outputs:
- probe_out: float32 [2, 1024, 1024], P(None, 'space')
- control_out: float32 [2, 1024, 1024], P(None, 'space')
- optical_out: float32 [2, 64, 1024, 1024], P(None, 'vel', 'space')
- spin_out: float32 [2, 64, 1024, 1024], P(None, 'vel', 'space')
The draws below stay inside these ranges and needn't reach their ends.
All inputs are finite; a program needn't handle non-finite values.
Results may differ from the reference program's by a relative error of at most 0.000098.
Values sent between devices are 32-bit elements; how exact they have to be, the bound alone decides.
A program may use at most 192 MiB of HBM per device.

```python
import math
import jax
import jax.numpy as jnp
from jax import lax

GRID = 1024
VEL = 64


def block_levels(key, dims, shards, least, high):
    loudness = 1.0
    for position, shards_of in shards:
        draws = jax.random.uniform(jax.random.fold_in(jax.random.fold_in(key, 6), position), (shards_of,), jnp.float32, least / len(shards), high / len(shards))
        loudness = loudness * jnp.repeat(jnp.exp(draws), dims[position] // shards_of).reshape((-1,) + (1,) * (len(dims) - 1 - position))
    return loudness


def scatter_about(key, extent, spread, reach, cuts=(), kind=jnp.bfloat16):
    level = block_levels(key, extent, cuts, -0.22, 0.18) if cuts else 1.0
    values = jax.random.normal(key, extent, jnp.float32) * spread * level
    return jnp.minimum(jnp.maximum(values, -reach), reach).astype(kind)


def setup_inputs(seed: int = 0) -> dict:
    seeds = jax.random.split(jax.random.key(seed), 8)
    return {
        "probe_field": scatter_about(seeds[0], (2, GRID, GRID), 1.0, 6.0, ((1, 8),), jnp.float32),
        "control_field": scatter_about(seeds[1], (2, GRID, GRID), 1.0, 4.0, ((1, 8),), jnp.float32),
        "optical_state": scatter_about(seeds[2], (2, VEL, GRID, GRID), 0.5, 3.0, ((1, 4), (2, 8)), jnp.float32),
        "spin_state": scatter_about(seeds[3], (2, VEL, GRID, GRID), 0.5, 3.0, ((1, 4), (2, 8)), jnp.float32),
        "doppler_shift": scatter_about(seeds[4], (VEL,), 1.0, 3.0, ((0, 4),), jnp.float32),
        "class_weight": jnp.clip(jnp.exp(math.log(2.0) - 2.3025851 * jax.random.uniform(seeds[5], (VEL,), jnp.float32) ** block_levels(seeds[5], (VEL,), ((0, 4),), -0.2, 0.2)), 0.2, 2.0),
        "gradient_shift": scatter_about(seeds[6], (GRID, GRID), 1.0, 3.0, ((0, 8),), jnp.float32),
    }


GAMMA = 1.0
DEPHASE = 0.1
DT = 0.25
COUPLE = 2.0


def phase_angles(grid_width):
    counter = jnp.arange(grid_width, dtype=jnp.int32)
    frequency = jnp.where(counter < grid_width // 2, counter, counter - grid_width)
    return jnp.pi * ((frequency * frequency) % (2 * grid_width)).astype(jnp.float32) / grid_width


def diffract(complex_field, phase_plane):
    wavefront = complex_field[0] + 1j * complex_field[1]
    result = jnp.fft.ifft2(jnp.fft.fft2(wavefront) * phase_plane)
    return jnp.stack([jnp.real(result), jnp.imag(result)]).astype(jnp.float32)


def derivative(optical, spin_part, probe_part, control, doppler, gradient):
    optical_real, optical_imag = optical[0], optical[1]
    spin_real, spin_imag = spin_part[0], spin_part[1]
    probe_real, probe_imag = probe_part[0], probe_part[1]
    control_real, control_imag = control[0], control[1]
    rate_optical_real = -GAMMA * optical_real + doppler * optical_imag - probe_imag - (control_real * spin_imag + control_imag * spin_real)
    rate_optical_imag = -GAMMA * optical_imag - doppler * optical_real + probe_real + (control_real * spin_real - control_imag * spin_imag)
    rate_spin_real = -DEPHASE * spin_real + gradient * spin_imag - (control_real * optical_imag - control_imag * optical_real)
    rate_spin_imag = -DEPHASE * spin_imag - gradient * spin_real + (control_real * optical_real + control_imag * optical_imag)
    return jnp.stack([rate_optical_real, rate_optical_imag]), jnp.stack([rate_spin_real, rate_spin_imag])


def midpoint(optical, spin_part, probe_part, control, doppler, gradient):
    rate_optical, rate_spin = derivative(optical, spin_part, probe_part, control, doppler, gradient)
    half_optical = optical + 0.5 * DT * rate_optical
    half_spin = spin_part + 0.5 * DT * rate_spin
    rate_optical, rate_spin = derivative(half_optical, half_spin, probe_part, control, doppler, gradient)
    return optical + DT * rate_optical, spin_part + DT * rate_spin


def reference(probe_field, control_field, optical_state, spin_state, doppler_shift, class_weight, gradient_shift):
    angles = phase_angles(GRID)
    phase_plane = jnp.exp(-1j * (angles[:, None] + angles[None, :]))
    probe_one = diffract(probe_field, phase_plane)
    control_one = diffract(control_field, phase_plane)
    optical_classes = jnp.moveaxis(optical_state, 1, 0)
    spin_classes = jnp.moveaxis(spin_state, 1, 0)

    def advance(class_item):
        optical, spin_part, doppler = class_item
        return midpoint(optical, spin_part, probe_one, control_one, doppler, gradient_shift)

    optical_new, spin_new = lax.map(advance, (optical_classes, spin_classes, doppler_shift))
    polarization = jnp.einsum('vcrn,v->crn', optical_new, class_weight, precision=lax.Precision.HIGHEST) / VEL
    probe_two = jnp.stack([probe_one[0] - COUPLE * polarization[1], probe_one[1] + COUPLE * polarization[0]])
    probe_out = diffract(probe_two, phase_plane)
    control_out = diffract(control_one, phase_plane)
    return probe_out, control_out, jnp.moveaxis(optical_new, 0, 1), jnp.moveaxis(spin_new, 0, 1)
```

```python
import functools
import jax
import jax.numpy as jnp
import numpy as np
from jax import lax
from jax.experimental import pallas as pl
from jax.experimental.pallas import tpu as pltpu
from jax.sharding import PartitionSpec as P

GAMMA = 1.0
DEPHASE = 0.1
DT = 0.25
COUPLE = 2.0
EXACT = lax.Precision.HIGH


def circulant_tables(grid_width):
    counter = np.arange(grid_width, dtype=np.int32)
    frequency = np.where(counter < grid_width // 2, counter, counter - grid_width)
    angles = (
        np.float32(np.pi)
        * (frequency * frequency % (2 * grid_width)).astype(np.float32)
        / np.float32(grid_width)
    )
    turns = counter[:, None] * counter[None, :] % grid_width
    argument = (
        np.float32(2.0 * np.pi) * turns.astype(np.float32) / np.float32(grid_width)
        - angles[None, :]
    )
    kernel_real = np.mean(np.cos(argument), axis=1)
    kernel_imag = np.mean(np.sin(argument), axis=1)
    offsets = (counter[:, None] - counter[None, :]) % grid_width
    return (kernel_real[offsets].astype(np.float32), kernel_imag[offsets].astype(np.float32))


def mix_left(table_real, table_imag, section):
    real_in, imag_in = (section[:, 0], section[:, 1])

    def product_of(table, values):
        return jnp.einsum("mn,fnk->fmk", table, values, precision=EXACT)

    return jnp.stack(
        [
            product_of(table_real, real_in) - product_of(table_imag, imag_in),
            product_of(table_real, imag_in) + product_of(table_imag, real_in),
        ],
        axis=1,
    )


def mix_right(section, table_real, table_imag):
    real_in, imag_in = (section[:, 0], section[:, 1])

    def product_of(values, table):
        return jnp.einsum("fmn,nk->fmk", values, table, precision=EXACT)

    return jnp.stack(
        [
            product_of(real_in, table_real) - product_of(imag_in, table_imag),
            product_of(imag_in, table_real) + product_of(real_in, table_imag),
        ],
        axis=1,
    )


def state_kernel(doppler_ref, weight_ref, probe_ref, control_ref, gradient_ref, optical_ref, spin_ref, optical_out, spin_out, total_ref, *, scale):
    classes = optical_ref.shape[1]
    width = optical_ref.shape[3]
    step = DT
    half = 0.5 * DT * DT

    def lane_block(block, carry):
        lanes = pl.ds(pl.multiple_of(block * 128, 128), 128)
        probe_real, probe_imag = probe_ref[0, :, lanes], probe_ref[1, :, lanes]
        control_real, control_imag = control_ref[0, :, lanes], control_ref[1, :, lanes]
        gradient = gradient_ref[:, lanes]
        power = half * (control_real * control_real + control_imag * control_imag)
        keep_real = step - half * (GAMMA + DEPHASE)
        keep_imag = -half * gradient
        into_real = -control_imag * keep_real - control_real * keep_imag
        into_imag = control_real * keep_real - control_imag * keep_imag
        back_real = control_imag * keep_real - control_real * keep_imag
        back_imag = control_real * keep_real + control_imag * keep_imag
        slope_real, slope_imag = half * control_real, half * control_imag
        source_real = -(step - half * GAMMA) * probe_imag
        source_imag = (step - half * GAMMA) * probe_real
        drive_real, drive_imag = half * probe_real, half * probe_imag
        spin_source_real = -half * (control_real * probe_real + control_imag * probe_imag)
        spin_source_imag = -half * (control_real * probe_imag - control_imag * probe_real)
        decay_real = 1.0 - step * DEPHASE + half * (DEPHASE * DEPHASE - gradient * gradient) - power
        decay_imag = (2.0 * half * DEPHASE - step) * gradient
        sum_real = jnp.zeros_like(gradient)
        sum_imag = jnp.zeros_like(gradient)
        for item in range(classes):
            shift = doppler_ref[item]
            weight = weight_ref[item] * scale
            self_real = (1.0 - step * GAMMA + half * (GAMMA * GAMMA - shift * shift)) - power
            self_imag = (2.0 * half * GAMMA - step) * shift
            turn_real, turn_imag = shift * slope_real, shift * slope_imag
            pull_real, pull_imag = into_real + turn_real, into_imag + turn_imag
            push_real, push_imag = back_real + turn_real, back_imag - turn_imag
            a_real, a_imag = optical_ref[0, item, :, lanes], optical_ref[1, item, :, lanes]
            b_real, b_imag = spin_ref[0, item, :, lanes], spin_ref[1, item, :, lanes]
            new_real = (
                self_real * a_real - self_imag * a_imag + pull_real * b_real - pull_imag * b_imag
                + (source_real + shift * drive_real)
            )
            new_imag = (
                self_real * a_imag + self_imag * a_real + pull_real * b_imag + pull_imag * b_real
                + (source_imag + shift * drive_imag)
            )
            optical_out[0, item, :, lanes] = new_real
            optical_out[1, item, :, lanes] = new_imag
            spin_out[0, item, :, lanes] = (
                push_real * a_real - push_imag * a_imag + decay_real * b_real - decay_imag * b_imag + spin_source_real
            )
            spin_out[1, item, :, lanes] = (
                push_real * a_imag + push_imag * a_real + decay_real * b_imag + decay_imag * b_real + spin_source_imag
            )
            sum_real += weight * new_real
            sum_imag += weight * new_imag
        total_ref[0, :, lanes] = sum_real
        total_ref[1, :, lanes] = sum_imag
        return carry

    lax.fori_loop(0, width // 128, lane_block, 0)


def advance(optical, spin_part, probe_part, control, doppler, weight, gradient, scale):
    _, classes, rows, width = optical.shape
    tall = 8
    state = pl.BlockSpec((2, classes, tall, width), lambda i: (0, 0, i, 0))
    plane = pl.BlockSpec((2, tall, width), lambda i: (0, i, 0))
    small = pl.BlockSpec(memory_space=pltpu.SMEM)
    return pl.pallas_call(
        functools.partial(state_kernel, scale=scale),
        grid=(rows // tall,),
        in_specs=[small, small, plane, plane, pl.BlockSpec((tall, width), lambda i: (i, 0)), state, state],
        out_specs=[state, state, plane],
        out_shape=[
            jax.ShapeDtypeStruct(optical.shape, jnp.float32),
            jax.ShapeDtypeStruct(spin_part.shape, jnp.float32),
            jax.ShapeDtypeStruct((2, rows, width), jnp.float32),
        ],
        compiler_params=pltpu.CompilerParams(vmem_limit_bytes=40 << 20),
        name="advance_states",
    )(doppler, weight, probe_part, control, gradient, optical, spin_part)


def add_source(complex_field, polarization):
    return jnp.stack(
        [complex_field[0] - COUPLE * polarization[1], complex_field[1] + COUPLE * polarization[0]]
    )


def shards(
    probe_field,
    control_field,
    optical_state,
    spin_state,
    doppler_shift,
    class_weight,
    gradient_shift,
):
    grid_width = probe_field.shape[2]
    quarter_width = grid_width // lax.axis_size("vel")
    table_real, table_imag = circulant_tables(grid_width)
    full_real = jnp.asarray(table_real)
    full_imag = jnp.asarray(table_imag)

    def row_mix(section):
        blended = mix_left(
            full_real,
            full_imag,
            lax.all_to_all(section, "space", split_axis=3, concat_axis=2, tiled=True),
        )
        return lax.all_to_all(blended, "space", split_axis=2, concat_axis=3, tiled=True)

    def spread(section):
        return lax.all_gather(section, "vel", axis=3, tiled=True)

    stacked = jnp.stack([probe_field, control_field])
    col_start = lax.axis_index("vel") * quarter_width
    quart_real = lax.dynamic_slice_in_dim(full_real, col_start, quarter_width, 1)
    quart_imag = lax.dynamic_slice_in_dim(full_imag, col_start, quarter_width, 1)
    stacked = spread(row_mix(mix_right(stacked, quart_real, quart_imag)))
    optical_new, spin_new, weighted = advance(
        optical_state,
        spin_state,
        stacked[0],
        stacked[1],
        doppler_shift,
        class_weight,
        gradient_shift,
        1.0 / (optical_state.shape[1] * lax.axis_size("vel")),
    )
    polarization = lax.psum_scatter(weighted, "vel", scatter_dimension=2, tiled=True)
    probe_part = lax.dynamic_slice_in_dim(stacked[0], col_start, quarter_width, 2)
    control_part = lax.dynamic_slice_in_dim(stacked[1], col_start, quarter_width, 2)
    section = jnp.stack([add_source(probe_part, polarization), control_part])
    stacked = mix_right(spread(row_mix(section)), full_real, full_imag)
    return (stacked[0], stacked[1], optical_new, spin_new)


def solution(mesh):
    return jax.shard_map(
        shards,
        mesh=mesh,
        in_specs=(
            P(None, "space", None),
            P(None, "space", None),
            P(None, "vel", "space", None),
            P(None, "vel", "space", None),
            P("vel"),
            P("vel"),
            P("space", None),
        ),
        out_specs=(
            P(None, "space", None),
            P(None, "space", None),
            P(None, "vel", "space", None),
            P(None, "vel", "space", None),
        ),
        check_vma=False,
    )
```

```python
import functools
import jax
import jax.numpy as jnp
import numpy as np
from jax import lax
from jax.experimental import pallas as pl
from jax.experimental.pallas import tpu as pltpu
from jax.sharding import PartitionSpec as P

GAMMA = 1.0
DEPHASE = 0.1
DT = 0.25
COUPLE = 2.0
BAND = 128
MESH = pl.DeviceIdType.MESH


def mixing_tables(width):
    counter = np.arange(width)
    frequency = np.where(counter < width // 2, counter, counter - width)
    angles = np.pi * (frequency * frequency % (2 * width)) / width
    kernel = np.fft.ifft(np.exp(-1j * angles))
    band = kernel[(np.arange(BAND)[:, None] - np.arange(2 * width)[None, :]) % width]
    full = np.stack([band.real, band.imag]).astype(np.float32)
    high = full.astype(jnp.bfloat16)
    low = (full - high.astype(np.float32)).astype(jnp.bfloat16)
    return jnp.asarray(np.stack([high, low], axis=1))


def split(values):
    high = values.astype(jnp.bfloat16)
    return high, (values - high.astype(jnp.float32)).astype(jnp.bfloat16)


def outer_dot(left, right):
    return lax.dot_general(left, right, (((1,), (1,)), ((), ())), preferred_element_type=jnp.float32)


def inner_dot(left, right):
    return jnp.dot(left, right, preferred_element_type=jnp.float32)


class Mixer:
    def __init__(self, spaces, groups, width, rows, table, scratch):
        self.spaces, self.groups, self.width, self.rows = spaces, groups, width, rows
        self.table = table
        (self.high, self.low, self.out_chunks, self.in_chunks, self.back_chunks, self.gathered,
         self.row_send, self.row_recv, self.back_send, self.back_recv,
         self.far_send, self.far_recv, self.core_send, self.core_recv) = scratch
        self.columns = width // groups
        self.piece = self.columns // spaces
        self.space = lax.axis_index("space")
        self.vel = lax.axis_index("vel")
        self.core = self.vel % 2
        self.far = self.vel // 2
        self.core_peer = self.far * 2 + 1 - self.core
        self.sent = []

    def far_peer(self, hop):
        return ((self.far + hop) % (self.groups // 2)) * 2 + self.core

    def enter(self):
        barrier = pltpu.get_barrier_semaphore()
        for hop in range(1, self.spaces):
            pl.semaphore_signal(barrier, inc=1, device_id={"space": (self.space + hop) % self.spaces}, device_id_type=MESH)
        for hop in range(1, self.groups // 2):
            pl.semaphore_signal(barrier, inc=1, device_id={"vel": self.far_peer(hop)}, device_id_type=MESH)
        pl.semaphore_signal(barrier, inc=1, device_id={"vel": self.core_peer}, device_id_type=MESH)
        pl.semaphore_wait(barrier, self.spaces - 1 + self.groups // 2)

    def push(self, source, target, send_sem, recv_sem, device):
        copy = pltpu.make_async_remote_copy(
            src_ref=source, dst_ref=target, send_sem=send_sem, recv_sem=recv_sem,
            device_id=device, device_id_type=MESH,
        )
        copy.start()
        self.sent.append(copy)
        return copy

    def columns_stage(self, field, real, imag):
        rows, piece, spaces = self.rows, self.piece, self.spaces
        for part, plane in enumerate((real, imag)):
            high, low = split(plane)
            self.high[part * rows:(part + 1) * rows, :] = high
            self.low[part * rows:(part + 1) * rows, :] = low
        products = []
        for part in range(2):
            bands = [[], []]
            for block in range(self.columns // BAND):
                start = self.width - self.vel * self.columns - block * BAND
                lanes = pl.ds(pl.multiple_of(start, BAND), self.width)
                for level in range(2):
                    bands[level].append(self.table[part, level, :, lanes])
            first = jnp.concatenate(bands[0], axis=0)
            both = outer_dot(jnp.concatenate(bands[0] + bands[1], axis=0), self.high[...])
            products.append(both[:self.columns] + both[self.columns:] + outer_dot(first, self.low[...]))
        mixed = (
            products[0][:, :rows] - products[1][:, rows:],
            products[0][:, rows:] + products[1][:, :rows],
        )
        for target in range(spaces):
            for part in range(2):
                self.out_chunks[field, target, part * piece:(part + 1) * piece, :] = mixed[part][target * piece:(target + 1) * piece]
        self.rows_in = getattr(self, "rows_in", {})
        self.rows_in[field] = []
        for hop in range(1, spaces):
            target = (self.space + hop) % spaces
            self.rows_in[field].append(self.push(
                self.out_chunks.at[field, target], self.in_chunks.at[field, self.space],
                self.row_send.at[field, hop], self.row_recv.at[field, hop], {"space": target},
            ))
        self.in_chunks[field, self.space] = self.out_chunks[field, self.space]

    def rows_stage(self, field):
        rows, piece, spaces, width = self.rows, self.piece, self.spaces, self.width
        for copy in self.rows_in[field]:
            copy.wait_recv()
        values = jnp.concatenate([self.in_chunks[field, source] for source in range(spaces)], axis=1)
        high, low = split(values)
        stacked = jnp.concatenate([high, low], axis=0)
        tile = 2 * BAND
        for start in range(0, width, tile):
            products = []
            for part in range(2):
                bands = [
                    jnp.concatenate([
                        self.table[part, level, :, width - block * BAND + start:width - block * BAND + start + tile]
                        if width - block * BAND + start + tile <= 2 * width
                        else self.table[part, level, :, start - block * BAND:start - block * BAND + tile]
                        for block in range(width // BAND)
                    ], axis=0)
                    for level in range(2)
                ]
                both = inner_dot(stacked, bands[0])
                products.append(both[:2 * piece] + both[2 * piece:] + inner_dot(high, bands[1]))
            real = products[0][:piece] - products[1][piece:]
            imag = products[0][piece:] + products[1][:piece]
            for offset in range(0, tile, rows):
                target = (start + offset) // rows
                self.back_chunks[field, target, :piece, :] = real[:, offset:offset + rows]
                self.back_chunks[field, target, piece:, :] = imag[:, offset:offset + rows]
        self.back_in = getattr(self, "back_in", {})
        self.back_in[field] = []
        for hop in range(1, spaces):
            target = (self.space + hop) % spaces
            self.back_in[field].append(self.push(
                self.back_chunks.at[field, target], self.gathered.at[field, self.vel, self.space],
                self.back_send.at[field, hop], self.back_recv.at[field, hop], {"space": target},
            ))
        self.gathered[field, self.vel, self.space] = self.back_chunks[field, self.space]

    def spread_stage(self, field):
        arrivals, core_copies = [], []
        for hop in range(self.spaces):
            source = (self.space + self.spaces - hop) % self.spaces
            if hop:
                self.back_in[field][hop - 1].wait_recv()
            chunk = self.gathered.at[field, self.vel, source]
            for far in range(1, self.groups // 2):
                arrivals.append((far, hop, self.push(
                    chunk, chunk, self.far_send.at[field, far, hop], self.far_recv.at[field, far, hop],
                    {"vel": self.far_peer(far)},
                )))
            core_copies.append(self.push(
                chunk, chunk, self.core_send.at[field, 0, hop], self.core_recv.at[field, 0, hop],
                {"vel": self.core_peer},
            ))
        for far, hop, copy in arrivals:
            copy.wait_recv()
            source = (self.space + self.spaces - hop) % self.spaces
            origin = self.far_peer(self.groups // 2 - far)
            chunk = self.gathered.at[field, origin, source]
            core_copies.append(self.push(
                chunk, chunk, self.core_send.at[field, far, hop], self.core_recv.at[field, far, hop],
                {"vel": self.core_peer},
            ))
        for copy in core_copies:
            copy.wait_recv()

    def finish(self, field, out_ref):
        piece = self.piece
        for start in range(0, self.width, BAND):
            group = start // self.columns
            first = (start % self.columns) // piece
            for part in range(2):
                block = jnp.concatenate([
                    self.gathered[field, group, source, part * piece:(part + 1) * piece, :]
                    for source in range(first, first + BAND // piece)
                ], axis=0)
                out_ref[part, :, start:start + BAND] = block.T

    def leave(self):
        for copy in self.sent:
            copy.wait_send()


def first_kernel(spaces, groups, probe_ref, control_ref, table_ref, probe_out, control_out, *scratch):
    _, rows, width = probe_ref.shape
    mixer = Mixer(spaces, groups, width, rows, table_ref, scratch)
    mixer.enter()
    mixer.columns_stage(0, probe_ref[0], probe_ref[1])
    mixer.columns_stage(1, control_ref[0], control_ref[1])
    mixer.rows_stage(0)
    mixer.rows_stage(1)
    mixer.spread_stage(0)
    mixer.finish(0, probe_out)
    mixer.spread_stage(1)
    mixer.finish(1, control_out)
    mixer.leave()


def second_kernel(spaces, groups, probe_ref, control_ref, part_ref, table_ref, probe_out, control_out,
                  core_part, far_parts, pair_sum, total, sum_send, sum_recv, *scratch):
    _, rows, width = probe_ref.shape
    mixer = Mixer(spaces, groups, width, rows, table_ref, scratch)
    core, peer = mixer.core, {"vel": mixer.core_peer}
    mixer.enter()
    swap = mixer.push(part_ref.at[1 - core], core_part, sum_send.at[0], sum_recv.at[0], peer)
    mixer.columns_stage(0, control_ref[0], control_ref[1])
    swap.wait_recv()
    pair_sum[...] = part_ref[core] + core_part[...]
    swaps = [
        mixer.push(pair_sum, far_parts.at[far], sum_send.at[1 + far], sum_recv.at[1 + far], {"vel": mixer.far_peer(far)})
        for far in range(1, groups // 2)
    ]
    mixer.rows_stage(0)
    whole = pair_sum[...]
    for far, copy in enumerate(swaps, 1):
        copy.wait_recv()
        whole = whole + far_parts[far]
    total[core] = whole
    swap = mixer.push(total.at[core], total.at[core], sum_send.at[1], sum_recv.at[1], peer)
    swap.wait_recv()
    mixer.columns_stage(1, probe_ref[0] - COUPLE * total[1], probe_ref[1] + COUPLE * total[0])
    mixer.spread_stage(0)
    mixer.rows_stage(1)
    mixer.finish(0, control_out)
    mixer.spread_stage(1)
    mixer.finish(1, probe_out)
    mixer.leave()


def diffract(kernel, spaces, groups, collective, fields, extra, table):
    _, rows, width = fields[0].shape
    piece = width // groups // spaces
    chunks = pltpu.VMEM((2, spaces, 2 * piece, rows), jnp.float32)
    dma = pltpu.SemaphoreType.DMA
    scratch = [
        pltpu.VMEM((2 * rows, width), jnp.bfloat16),
        pltpu.VMEM((2 * rows, width), jnp.bfloat16),
        chunks, chunks, chunks,
        pltpu.VMEM((2, groups, spaces, 2 * piece, rows), jnp.float32),
        dma((2, spaces)), dma((2, spaces)), dma((2, spaces)), dma((2, spaces)),
        dma((2, groups // 2, spaces)), dma((2, groups // 2, spaces)),
        dma((2, groups // 2, spaces)), dma((2, groups // 2, spaces)),
    ]
    if extra:
        plane = pltpu.VMEM((rows, width), jnp.float32)
        scratch = [
            plane, pltpu.VMEM((groups // 2, rows, width), jnp.float32), plane,
            pltpu.VMEM((2, rows, width), jnp.float32),
            dma((1 + groups // 2,)), dma((1 + groups // 2,)),
        ] + scratch
    operands = (*fields, *extra, table)
    vmem = pl.BlockSpec(memory_space=pltpu.VMEM)
    shape = jax.ShapeDtypeStruct(fields[0].shape, jnp.float32)
    return pl.pallas_call(
        functools.partial(kernel, spaces, groups),
        in_specs=[vmem] * len(operands),
        out_specs=[vmem, vmem],
        out_shape=[shape, shape],
        scratch_shapes=scratch,
        compiler_params=pltpu.CompilerParams(collective_id=collective, has_side_effects=True, vmem_limit_bytes=56 << 20),
        name=kernel.__name__,
    )(*operands)


def state_kernel(doppler_ref, weight_ref, probe_ref, control_ref, gradient_ref, optical_ref, spin_ref, optical_out, spin_out, total_ref, *, scale):
    classes = optical_ref.shape[1]
    width = optical_ref.shape[3]
    step = DT
    half = 0.5 * DT * DT

    def lane_block(block, carry):
        lanes = pl.ds(pl.multiple_of(block * 128, 128), 128)
        probe_real, probe_imag = probe_ref[0, :, lanes], probe_ref[1, :, lanes]
        control_real, control_imag = control_ref[0, :, lanes], control_ref[1, :, lanes]
        gradient = gradient_ref[:, lanes]
        power = half * (control_real * control_real + control_imag * control_imag)
        keep_real = step - half * (GAMMA + DEPHASE)
        keep_imag = -half * gradient
        into_real = -control_imag * keep_real - control_real * keep_imag
        into_imag = control_real * keep_real - control_imag * keep_imag
        back_real = control_imag * keep_real - control_real * keep_imag
        back_imag = control_real * keep_real + control_imag * keep_imag
        slope_real, slope_imag = half * control_real, half * control_imag
        source_real = -(step - half * GAMMA) * probe_imag
        source_imag = (step - half * GAMMA) * probe_real
        drive_real, drive_imag = half * probe_real, half * probe_imag
        spin_source_real = -half * (control_real * probe_real + control_imag * probe_imag)
        spin_source_imag = -half * (control_real * probe_imag - control_imag * probe_real)
        decay_real = 1.0 - step * DEPHASE + half * (DEPHASE * DEPHASE - gradient * gradient) - power
        decay_imag = (2.0 * half * DEPHASE - step) * gradient
        sum_real = jnp.zeros_like(gradient)
        sum_imag = jnp.zeros_like(gradient)
        for item in range(classes):
            shift = doppler_ref[item]
            weight = weight_ref[item] * scale
            self_real = (1.0 - step * GAMMA + half * (GAMMA * GAMMA - shift * shift)) - power
            self_imag = (2.0 * half * GAMMA - step) * shift
            turn_real, turn_imag = shift * slope_real, shift * slope_imag
            pull_real, pull_imag = into_real + turn_real, into_imag + turn_imag
            push_real, push_imag = back_real + turn_real, back_imag - turn_imag
            a_real, a_imag = optical_ref[0, item, :, lanes], optical_ref[1, item, :, lanes]
            b_real, b_imag = spin_ref[0, item, :, lanes], spin_ref[1, item, :, lanes]
            new_real = (
                self_real * a_real - self_imag * a_imag + pull_real * b_real - pull_imag * b_imag
                + (source_real + shift * drive_real)
            )
            new_imag = (
                self_real * a_imag + self_imag * a_real + pull_real * b_imag + pull_imag * b_real
                + (source_imag + shift * drive_imag)
            )
            optical_out[0, item, :, lanes] = new_real
            optical_out[1, item, :, lanes] = new_imag
            spin_out[0, item, :, lanes] = (
                push_real * a_real - push_imag * a_imag + decay_real * b_real - decay_imag * b_imag + spin_source_real
            )
            spin_out[1, item, :, lanes] = (
                push_real * a_imag + push_imag * a_real + decay_real * b_imag + decay_imag * b_real + spin_source_imag
            )
            sum_real += weight * new_real
            sum_imag += weight * new_imag
        total_ref[0, :, lanes] = sum_real
        total_ref[1, :, lanes] = sum_imag
        return carry

    lax.fori_loop(0, width // 128, lane_block, 0)


def advance(optical, spin_part, probe_part, control, doppler, weight, gradient, scale):
    _, classes, rows, width = optical.shape
    tall = 8
    state = pl.BlockSpec((2, classes, tall, width), lambda i: (0, 0, i, 0))
    plane = pl.BlockSpec((2, tall, width), lambda i: (0, i, 0))
    small = pl.BlockSpec(memory_space=pltpu.SMEM)
    return pl.pallas_call(
        functools.partial(state_kernel, scale=scale),
        grid=(rows // tall,),
        in_specs=[small, small, plane, plane, pl.BlockSpec((tall, width), lambda i: (i, 0)), state, state],
        out_specs=[state, state, plane],
        out_shape=[
            jax.ShapeDtypeStruct(optical.shape, jnp.float32),
            jax.ShapeDtypeStruct(spin_part.shape, jnp.float32),
            jax.ShapeDtypeStruct((2, rows, width), jnp.float32),
        ],
        compiler_params=pltpu.CompilerParams(vmem_limit_bytes=40 << 20),
        name="advance_states",
    )(doppler, weight, probe_part, control, gradient, optical, spin_part)


def shards(
    spaces,
    groups,
    probe_field,
    control_field,
    optical_state,
    spin_state,
    doppler_shift,
    class_weight,
    gradient_shift,
):
    table = mixing_tables(probe_field.shape[2])
    probe_one, control_one = diffract(first_kernel, spaces, groups, 0, (probe_field, control_field), (), table)
    optical_new, spin_new, weighted = advance(
        optical_state,
        spin_state,
        probe_one,
        control_one,
        doppler_shift,
        class_weight,
        gradient_shift,
        1.0 / (optical_state.shape[1] * groups),
    )
    probe_out, control_out = diffract(second_kernel, spaces, groups, 1, (probe_one, control_one), (weighted,), table)
    return (probe_out, control_out, optical_new, spin_new)


def solution(mesh):
    return jax.shard_map(
        functools.partial(shards, mesh.shape["space"], mesh.shape["vel"]),
        mesh=mesh,
        in_specs=(
            P(None, "space", None),
            P(None, "space", None),
            P(None, "vel", "space", None),
            P(None, "vel", "space", None),
            P("vel"),
            P("vel"),
            P("space", None),
        ),
        out_specs=(
            P(None, "space", None),
            P(None, "space", None),
            P(None, "vel", "space", None),
            P(None, "vel", "space", None),
        ),
        check_vma=False,
    )
```

```python
import functools
import jax
import jax.numpy as jnp
import numpy as np
from jax import lax
from jax.experimental import pallas as pl
from jax.experimental.pallas import tpu as pltpu
from jax.sharding import PartitionSpec as P

GAMMA = 1.0
DEPHASE = 0.1
DT = 0.25
COUPLE = 2.0
BAND = 128
MESH = pl.DeviceIdType.MESH


def mixing_tables(width):
    counter = np.arange(width)
    frequency = np.where(counter < width // 2, counter, counter - width)
    angles = np.pi * (frequency * frequency % (2 * width)) / width
    kernel = np.fft.ifft(np.exp(-1j * angles))
    band = kernel[(np.arange(BAND)[:, None] - np.arange(2 * width)[None, :]) % width]
    full = np.stack([band.real, band.imag]).astype(np.float32)
    high = full.astype(jnp.bfloat16)
    low = (full - high.astype(np.float32)).astype(jnp.bfloat16)
    return jnp.asarray(np.stack([high, low], axis=1))


def split(values):
    high = values.astype(jnp.bfloat16)
    return high, (values - high.astype(jnp.float32)).astype(jnp.bfloat16)


def outer_dot(left, right):
    return lax.dot_general(left, right, (((1,), (1,)), ((), ())), preferred_element_type=jnp.float32)


def inner_dot(left, right):
    return jnp.dot(left, right, preferred_element_type=jnp.float32)


class Mixer:
    def __init__(self, spaces, groups, width, rows, table, scratch):
        self.spaces, self.groups, self.width, self.rows = spaces, groups, width, rows
        self.table = table
        (self.high, self.low, self.out_chunks, self.in_chunks, self.back_chunks, self.gathered,
         self.row_send, self.row_recv, self.back_send, self.back_recv,
         self.far_send, self.far_recv, self.core_send, self.core_recv) = scratch
        self.columns = width // groups
        self.piece = self.columns // spaces
        self.space = lax.axis_index("space")
        self.vel = lax.axis_index("vel")
        self.core = self.vel % 2
        self.far = self.vel // 2
        self.core_peer = self.far * 2 + 1 - self.core
        self.sent = []

    def far_peer(self, hop):
        return ((self.far + hop) % (self.groups // 2)) * 2 + self.core

    def enter(self):
        barrier = pltpu.get_barrier_semaphore()
        for hop in range(1, self.spaces):
            pl.semaphore_signal(barrier, inc=1, device_id={"space": (self.space + hop) % self.spaces}, device_id_type=MESH)
        for hop in range(1, self.groups // 2):
            pl.semaphore_signal(barrier, inc=1, device_id={"vel": self.far_peer(hop)}, device_id_type=MESH)
        pl.semaphore_signal(barrier, inc=1, device_id={"vel": self.core_peer}, device_id_type=MESH)
        pl.semaphore_wait(barrier, self.spaces - 1 + self.groups // 2)

    def push(self, source, target, send_sem, recv_sem, device):
        copy = pltpu.make_async_remote_copy(
            src_ref=source, dst_ref=target, send_sem=send_sem, recv_sem=recv_sem,
            device_id=device, device_id_type=MESH,
        )
        copy.start()
        self.sent.append(copy)
        return copy

    def columns_mix(self, vel, real, imag):
        rows = self.rows
        for part, plane in enumerate((real, imag)):
            high, low = split(plane)
            self.high[part * rows:(part + 1) * rows, :] = high
            self.low[part * rows:(part + 1) * rows, :] = low
        products = []
        for part in range(2):
            bands = [[], []]
            for block in range(self.columns // BAND):
                start = self.width - vel * self.columns - block * BAND
                lanes = pl.ds(pl.multiple_of(start, BAND), self.width)
                for level in range(2):
                    bands[level].append(self.table[part, level, :, lanes])
            first = jnp.concatenate(bands[0], axis=0)
            both = outer_dot(jnp.concatenate(bands[0] + bands[1], axis=0), self.high[...])
            products.append(both[:self.columns] + both[self.columns:] + outer_dot(first, self.low[...]))
        return (
            products[0][:, :rows] - products[1][:, rows:],
            products[0][:, rows:] + products[1][:, :rows],
        )

    def columns_stage(self, field, mixed):
        piece, spaces = self.piece, self.spaces
        for target in range(spaces):
            for part in range(2):
                self.out_chunks[field, target, part * piece:(part + 1) * piece, :] = mixed[part][target * piece:(target + 1) * piece]
        self.rows_in = getattr(self, "rows_in", {})
        self.rows_in[field] = []
        for hop in range(1, spaces):
            target = (self.space + hop) % spaces
            self.rows_in[field].append(self.push(
                self.out_chunks.at[field, target], self.in_chunks.at[field, self.space],
                self.row_send.at[field, hop], self.row_recv.at[field, hop], {"space": target},
            ))
        self.in_chunks[field, self.space] = self.out_chunks[field, self.space]

    def rows_stage(self, field):
        rows, piece, spaces, width = self.rows, self.piece, self.spaces, self.width
        for copy in self.rows_in[field]:
            copy.wait_recv()
        values = jnp.concatenate([self.in_chunks[field, source] for source in range(spaces)], axis=1)
        high, low = split(values)
        stacked = jnp.concatenate([high, low], axis=0)
        tile = 2 * BAND
        for start in range(0, width, tile):
            products = []
            for part in range(2):
                bands = [
                    jnp.concatenate([
                        self.table[part, level, :, width - block * BAND + start:width - block * BAND + start + tile]
                        if width - block * BAND + start + tile <= 2 * width
                        else self.table[part, level, :, start - block * BAND:start - block * BAND + tile]
                        for block in range(width // BAND)
                    ], axis=0)
                    for level in range(2)
                ]
                both = inner_dot(stacked, bands[0])
                products.append(both[:2 * piece] + both[2 * piece:] + inner_dot(high, bands[1]))
            real = products[0][:piece] - products[1][piece:]
            imag = products[0][piece:] + products[1][:piece]
            for offset in range(0, tile, rows):
                target = (start + offset) // rows
                self.back_chunks[field, target, :piece, :] = real[:, offset:offset + rows]
                self.back_chunks[field, target, piece:, :] = imag[:, offset:offset + rows]
        self.back_in = getattr(self, "back_in", {})
        self.back_in[field] = []
        for hop in range(1, spaces):
            target = (self.space + hop) % spaces
            self.back_in[field].append(self.push(
                self.back_chunks.at[field, target], self.gathered.at[field, self.vel, self.space],
                self.back_send.at[field, hop], self.back_recv.at[field, hop], {"space": target},
            ))
        self.gathered[field, self.vel, self.space] = self.back_chunks[field, self.space]

    def spread_stage(self, field):
        arrivals, core_copies = [], []
        for hop in range(self.spaces):
            source = (self.space + self.spaces - hop) % self.spaces
            if hop:
                self.back_in[field][hop - 1].wait_recv()
            chunk = self.gathered.at[field, self.vel, source]
            for far in range(1, self.groups // 2):
                arrivals.append((far, hop, self.push(
                    chunk, chunk, self.far_send.at[field, far, hop], self.far_recv.at[field, far, hop],
                    {"vel": self.far_peer(far)},
                )))
            core_copies.append(self.push(
                chunk, chunk, self.core_send.at[field, 0, hop], self.core_recv.at[field, 0, hop],
                {"vel": self.core_peer},
            ))
        for far, hop, copy in arrivals:
            copy.wait_recv()
            source = (self.space + self.spaces - hop) % self.spaces
            origin = self.far_peer(self.groups // 2 - far)
            chunk = self.gathered.at[field, origin, source]
            core_copies.append(self.push(
                chunk, chunk, self.core_send.at[field, far, hop], self.core_recv.at[field, far, hop],
                {"vel": self.core_peer},
            ))
        for copy in core_copies:
            copy.wait_recv()

    def finish(self, field, out_ref):
        piece = self.piece
        for start in range(0, self.width, BAND):
            group = start // self.columns
            first = (start % self.columns) // piece
            for part in range(2):
                block = jnp.concatenate([
                    self.gathered[field, group, source, part * piece:(part + 1) * piece, :]
                    for source in range(first, first + BAND // piece)
                ], axis=0)
                out_ref[part, :, start:start + BAND] = block.T

    def leave(self):
        for copy in self.sent:
            copy.wait_send()


def first_kernel(spaces, groups, probe_ref, control_ref, table_ref, probe_out, control_out, *scratch):
    _, rows, width = probe_ref.shape
    mixer = Mixer(spaces, groups, width, rows, table_ref, scratch)
    mixer.enter()
    mixer.columns_stage(0, mixer.columns_mix(mixer.vel, probe_ref[0], probe_ref[1]))
    mixer.columns_stage(1, mixer.columns_mix(mixer.vel, control_ref[0], control_ref[1]))
    mixer.rows_stage(0)
    mixer.rows_stage(1)
    mixer.spread_stage(0)
    mixer.finish(0, probe_out)
    mixer.spread_stage(1)
    mixer.finish(1, control_out)
    mixer.leave()


def second_kernel(spaces, groups, probe_ref, control_ref, part_ref, table_ref, chunks_out,
                  core_part, own_mix, far_mix, far_in, sum_send, sum_recv, out_sems, *scratch):
    _, rows, width = probe_ref.shape
    mixer = Mixer(spaces, groups, width, rows, table_ref, scratch)
    mixer.enter()
    swap = mixer.push(part_ref, core_part, sum_send.at[0], sum_recv.at[0], {"vel": mixer.core_peer})
    mixer.columns_stage(0, mixer.columns_mix(mixer.vel, control_ref[0], control_ref[1]))
    swap.wait_recv()
    core_part[...] = COUPLE * (core_part[...] + part_ref[...])
    swaps = []
    for far in range(1, groups // 2):
        real, imag = mixer.columns_mix(mixer.far_peer(far), -core_part[1], core_part[0])
        far_mix[far, 0] = real
        far_mix[far, 1] = imag
        swaps.append(mixer.push(
            far_mix.at[far], far_in.at[far], sum_send.at[far], sum_recv.at[far], {"vel": mixer.far_peer(far)},
        ))
    real, imag = mixer.columns_mix(mixer.vel, probe_ref[0] - core_part[1], probe_ref[1] + core_part[0])
    own_mix[0] = real
    own_mix[1] = imag
    mixer.rows_stage(0)
    whole = [own_mix[0], own_mix[1]]
    for far, copy in enumerate(swaps, 1):
        copy.wait_recv()
        whole = [whole[0] + far_in[far, 0], whole[1] + far_in[far, 1]]
    mixer.columns_stage(1, whole)
    mixer.spread_stage(0)
    control_copy = pltpu.make_async_copy(mixer.gathered.at[0], chunks_out.at[0], out_sems.at[0])
    control_copy.start()
    mixer.rows_stage(1)
    mixer.spread_stage(1)
    probe_copy = pltpu.make_async_copy(mixer.gathered.at[1], chunks_out.at[1], out_sems.at[1])
    probe_copy.start()
    mixer.leave()
    control_copy.wait()
    probe_copy.wait()


def assemble_kernel(chunks_ref, control_out, probe_out):
    _, _, spaces, tall, _ = chunks_ref.shape
    piece = tall // 2
    for field, out_ref in enumerate((control_out, probe_out)):
        for start in range(0, spaces * piece, BAND):
            for part in range(2):
                block = jnp.concatenate([
                    chunks_ref[field, 0, source, part * piece:(part + 1) * piece, :]
                    for source in range(start // piece, (start + BAND) // piece)
                ], axis=0)
                out_ref[part, :, start:start + BAND] = block.T


def assemble(chunks):
    _, groups, spaces, tall, rows = chunks.shape
    columns = spaces * tall // 2
    shape = jax.ShapeDtypeStruct((2, rows, groups * columns), jnp.float32)
    out = pl.BlockSpec((2, rows, columns), lambda i: (0, 0, i))
    return pl.pallas_call(
        assemble_kernel,
        grid=(groups,),
        in_specs=[pl.BlockSpec((2, 1, spaces, tall, rows), lambda i: (0, i, 0, 0, 0))],
        out_specs=[out, out],
        out_shape=[shape, shape],
        compiler_params=pltpu.CompilerParams(vmem_limit_bytes=60 * 1024 * 1024),
        name="assemble_fields",
    )(chunks)


def diffract(kernel, spaces, groups, collective, fields, extra, table):
    _, rows, width = fields[0].shape
    piece = width // groups // spaces
    chunks = pltpu.VMEM((2, spaces, 2 * piece, rows), jnp.float32)
    dma = pltpu.SemaphoreType.DMA
    scratch = [
        pltpu.VMEM((2 * rows, width), jnp.bfloat16),
        pltpu.VMEM((2 * rows, width), jnp.bfloat16),
        chunks, chunks, chunks,
        pltpu.VMEM((2, groups, spaces, 2 * piece, rows), jnp.float32),
        dma((2, spaces)), dma((2, spaces)), dma((2, spaces)), dma((2, spaces)),
        dma((2, groups // 2, spaces)), dma((2, groups // 2, spaces)),
        dma((2, groups // 2, spaces)), dma((2, groups // 2, spaces)),
    ]
    shape = jax.ShapeDtypeStruct(fields[0].shape, jnp.float32)
    vmem = pl.BlockSpec(memory_space=pltpu.VMEM)
    out_shape, out_specs = [shape, shape], [vmem, vmem]
    if extra:
        mixes = pltpu.VMEM((groups // 2, 2, width // groups, rows), jnp.float32)
        scratch = [
            pltpu.VMEM((2, rows, width), jnp.float32),
            pltpu.VMEM((2, width // groups, rows), jnp.float32), mixes, mixes,
            dma((groups // 2,)), dma((groups // 2,)), dma((2,)),
        ] + scratch
        out_shape = jax.ShapeDtypeStruct((2, groups, spaces, 2 * piece, rows), jnp.float32)
        out_specs = pl.BlockSpec(memory_space=pl.ANY)
    operands = (*fields, *extra, table)
    return pl.pallas_call(
        functools.partial(kernel, spaces, groups),
        in_specs=[vmem] * len(operands),
        out_specs=out_specs,
        out_shape=out_shape,
        scratch_shapes=scratch,
        compiler_params=pltpu.CompilerParams(collective_id=collective, has_side_effects=True, vmem_limit_bytes=60 * 1024 * 1024),
        name=kernel.__name__,
    )(*operands)


def state_kernel(doppler_ref, weight_ref, probe_ref, control_ref, gradient_ref, optical_ref, spin_ref, optical_out, spin_out, total_ref, *, scale):
    classes = optical_ref.shape[1]
    width = optical_ref.shape[3]
    step = DT
    half = 0.5 * DT * DT

    def lane_block(block, carry):
        lanes = pl.ds(pl.multiple_of(block * 128, 128), 128)
        probe_real, probe_imag = probe_ref[0, :, lanes], probe_ref[1, :, lanes]
        control_real, control_imag = control_ref[0, :, lanes], control_ref[1, :, lanes]
        gradient = gradient_ref[:, lanes]
        power = half * (control_real * control_real + control_imag * control_imag)
        keep_real = step - half * (GAMMA + DEPHASE)
        keep_imag = -half * gradient
        into_real = -control_imag * keep_real - control_real * keep_imag
        into_imag = control_real * keep_real - control_imag * keep_imag
        back_real = control_imag * keep_real - control_real * keep_imag
        back_imag = control_real * keep_real + control_imag * keep_imag
        slope_real, slope_imag = half * control_real, half * control_imag
        source_real = -(step - half * GAMMA) * probe_imag
        source_imag = (step - half * GAMMA) * probe_real
        drive_real, drive_imag = half * probe_real, half * probe_imag
        spin_source_real = -half * (control_real * probe_real + control_imag * probe_imag)
        spin_source_imag = -half * (control_real * probe_imag - control_imag * probe_real)
        decay_real = 1.0 - step * DEPHASE + half * (DEPHASE * DEPHASE - gradient * gradient) - power
        decay_imag = (2.0 * half * DEPHASE - step) * gradient
        sum_real = jnp.zeros_like(gradient)
        sum_imag = jnp.zeros_like(gradient)
        for item in range(classes):
            shift = doppler_ref[item]
            weight = weight_ref[item] * scale
            self_real = (1.0 - step * GAMMA + half * (GAMMA * GAMMA - shift * shift)) - power
            self_imag = (2.0 * half * GAMMA - step) * shift
            turn_real, turn_imag = shift * slope_real, shift * slope_imag
            pull_real, pull_imag = into_real + turn_real, into_imag + turn_imag
            push_real, push_imag = back_real + turn_real, back_imag - turn_imag
            a_real, a_imag = optical_ref[0, item, :, lanes], optical_ref[1, item, :, lanes]
            b_real, b_imag = spin_ref[0, item, :, lanes], spin_ref[1, item, :, lanes]
            new_real = (
                self_real * a_real - self_imag * a_imag + pull_real * b_real - pull_imag * b_imag
                + (source_real + shift * drive_real)
            )
            new_imag = (
                self_real * a_imag + self_imag * a_real + pull_real * b_imag + pull_imag * b_real
                + (source_imag + shift * drive_imag)
            )
            optical_out[0, item, :, lanes] = new_real
            optical_out[1, item, :, lanes] = new_imag
            spin_out[0, item, :, lanes] = (
                push_real * a_real - push_imag * a_imag + decay_real * b_real - decay_imag * b_imag + spin_source_real
            )
            spin_out[1, item, :, lanes] = (
                push_real * a_imag + push_imag * a_real + decay_real * b_imag + decay_imag * b_real + spin_source_imag
            )
            sum_real += weight * new_real
            sum_imag += weight * new_imag
        total_ref[0, :, lanes] = sum_real
        total_ref[1, :, lanes] = sum_imag
        return carry

    lax.fori_loop(0, width // 128, lane_block, 0)


def advance(optical, spin_part, probe_part, control, doppler, weight, gradient, scale):
    _, classes, rows, width = optical.shape
    tall = min(16, rows)
    state = pl.BlockSpec((2, classes, tall, width), lambda i: (0, 0, i, 0))
    plane = pl.BlockSpec((2, tall, width), lambda i: (0, i, 0))
    small = pl.BlockSpec(memory_space=pltpu.SMEM)
    return pl.pallas_call(
        functools.partial(state_kernel, scale=scale),
        grid=(rows // tall,),
        in_specs=[small, small, plane, plane, pl.BlockSpec((tall, width), lambda i: (i, 0)), state, state],
        out_specs=[state, state, plane],
        out_shape=[
            jax.ShapeDtypeStruct(optical.shape, jnp.float32),
            jax.ShapeDtypeStruct(spin_part.shape, jnp.float32),
            jax.ShapeDtypeStruct((2, rows, width), jnp.float32),
        ],
        compiler_params=pltpu.CompilerParams(vmem_limit_bytes=60 * 1024 * 1024),
        name="advance_states",
    )(doppler, weight, probe_part, control, gradient, optical, spin_part)


def shards(
    spaces,
    groups,
    probe_field,
    control_field,
    optical_state,
    spin_state,
    doppler_shift,
    class_weight,
    gradient_shift,
):
    table = mixing_tables(probe_field.shape[2])
    probe_one, control_one = diffract(first_kernel, spaces, groups, 0, (probe_field, control_field), (), table)
    optical_new, spin_new, weighted = advance(
        optical_state,
        spin_state,
        probe_one,
        control_one,
        doppler_shift,
        class_weight,
        gradient_shift,
        1.0 / (optical_state.shape[1] * groups),
    )
    control_out, probe_out = assemble(diffract(second_kernel, spaces, groups, 1, (probe_one, control_one), (weighted,), table))
    return (probe_out, control_out, optical_new, spin_new)


def solution(mesh):
    return jax.shard_map(
        functools.partial(shards, mesh.shape["space"], mesh.shape["vel"]),
        mesh=mesh,
        in_specs=(
            P(None, "space", None),
            P(None, "space", None),
            P(None, "vel", "space", None),
            P(None, "vel", "space", None),
            P("vel"),
            P("vel"),
            P("space", None),
        ),
        out_specs=(
            P(None, "space", None),
            P(None, "space", None),
            P(None, "vel", "space", None),
            P(None, "vel", "space", None),
        ),
        check_vma=False,
    )
```

```python
import functools
import jax
import jax.numpy as jnp
import numpy as np
from jax import lax
from jax.experimental import pallas as pl
from jax.experimental.pallas import tpu as pltpu
from jax.sharding import PartitionSpec as P

GAMMA = 1.0
DEPHASE = 0.1
DT = 0.25
COUPLE = 2.0
BAND = 128
MESH = pl.DeviceIdType.MESH


def mixing_tables(width):
    counter = np.arange(width)
    frequency = np.where(counter < width // 2, counter, counter - width)
    angles = np.pi * (frequency * frequency % (2 * width)) / width
    kernel = np.fft.ifft(np.exp(-1j * angles))
    band = kernel[(np.arange(BAND)[:, None] - np.arange(2 * width)[None, :]) % width]
    full = np.stack([band.real, band.imag]).astype(np.float32)
    high = full.astype(jnp.bfloat16)
    low = (full - high.astype(np.float32)).astype(jnp.bfloat16)
    return jnp.asarray(np.stack([high, low], axis=1))


def split(values):
    high = values.astype(jnp.bfloat16)
    return high, (values - high.astype(jnp.float32)).astype(jnp.bfloat16)


def outer_dot(left, right):
    return lax.dot_general(left, right, (((1,), (1,)), ((), ())), preferred_element_type=jnp.float32)


def inner_dot(left, right):
    return jnp.dot(left, right, preferred_element_type=jnp.float32)


class Mixer:
    def __init__(self, spaces, groups, width, rows, table, scratch):
        self.spaces, self.groups, self.width, self.rows = spaces, groups, width, rows
        self.table = table
        (self.high, self.low, self.out_chunks, self.in_chunks, self.back_chunks, self.gathered,
         self.row_send, self.row_recv, self.back_send, self.back_recv,
         self.far_send, self.far_recv, self.core_send, self.core_recv) = scratch
        self.columns = width // groups
        self.piece = self.columns // spaces
        self.space = lax.axis_index("space")
        self.vel = lax.axis_index("vel")
        self.core = self.vel % 2
        self.far = self.vel // 2
        self.core_peer = self.far * 2 + 1 - self.core
        self.sent = []

    def far_peer(self, hop):
        return ((self.far + hop) % (self.groups // 2)) * 2 + self.core

    def back_source(self, hop):
        members = 2 * BAND // self.rows
        turns = self.spaces // members
        turn, step = hop // members, hop % members
        tile_index = (self.space // members + turns - turn) % turns
        return tile_index * members + (self.space + members - step) % members

    def enter(self):
        barrier = pltpu.get_barrier_semaphore()
        for hop in range(1, self.spaces):
            pl.semaphore_signal(barrier, inc=1, device_id={"space": (self.space + hop) % self.spaces}, device_id_type=MESH)
        for hop in range(1, self.groups // 2):
            pl.semaphore_signal(barrier, inc=1, device_id={"vel": self.far_peer(hop)}, device_id_type=MESH)
        pl.semaphore_signal(barrier, inc=1, device_id={"vel": self.core_peer}, device_id_type=MESH)
        pl.semaphore_wait(barrier, self.spaces - 1 + self.groups // 2)

    def push(self, source, target, send_sem, recv_sem, device):
        copy = pltpu.make_async_remote_copy(
            src_ref=source, dst_ref=target, send_sem=send_sem, recv_sem=recv_sem,
            device_id=device, device_id_type=MESH,
        )
        copy.start()
        self.sent.append(copy)
        return copy

    def columns_mix(self, vel, real, imag):
        rows = self.rows
        for part, plane in enumerate((real, imag)):
            high, low = split(plane)
            self.high[part * rows:(part + 1) * rows, :] = high
            self.low[part * rows:(part + 1) * rows, :] = low
        products = []
        for part in range(2):
            bands = [[], []]
            for block in range(self.columns // BAND):
                start = self.width - vel * self.columns - block * BAND
                lanes = pl.ds(pl.multiple_of(start, BAND), self.width)
                for level in range(2):
                    bands[level].append(self.table[part, level, :, lanes])
            first = jnp.concatenate(bands[0], axis=0)
            both = outer_dot(jnp.concatenate(bands[0] + bands[1], axis=0), self.high[...])
            products.append(both[:self.columns] + both[self.columns:] + outer_dot(first, self.low[...]))
        return (
            products[0][:, :rows] - products[1][:, rows:],
            products[0][:, rows:] + products[1][:, :rows],
        )

    def columns_stage(self, field, mixed):
        piece, spaces = self.piece, self.spaces
        for target in range(spaces):
            for part in range(2):
                self.out_chunks[field, target, part * piece:(part + 1) * piece, :] = mixed[part][target * piece:(target + 1) * piece]
        self.rows_in = getattr(self, "rows_in", {})
        self.rows_in[field] = []
        for hop in range(1, spaces):
            target = (self.space + hop) % spaces
            self.rows_in[field].append(self.push(
                self.out_chunks.at[field, target], self.in_chunks.at[field, self.space],
                self.row_send.at[field, hop], self.row_recv.at[field, hop], {"space": target},
            ))
        self.in_chunks[field, self.space] = self.out_chunks[field, self.space]

    def rows_stage(self, field):
        rows, piece, spaces, width = self.rows, self.piece, self.spaces, self.width
        for copy in self.rows_in[field]:
            copy.wait_recv()
        values = jnp.concatenate([self.in_chunks[field, source] for source in range(spaces)], axis=1)
        high, low = split(values)
        stacked = jnp.concatenate([high, low], axis=0)
        tile = 2 * BAND
        members = tile // rows
        self.back_in = getattr(self, "back_in", {})
        self.back_in[field] = [None]
        for turn in range(width // tile):
            tile_index = (self.space // members + turn) % (width // tile)
            products = []
            for part in range(2):
                bands = [
                    jnp.concatenate([
                        self.table[part, level, :, pl.ds(pl.multiple_of(width - block * BAND + tile_index * tile, BAND), tile)]
                        for block in range(width // BAND)
                    ], axis=0)
                    for level in range(2)
                ]
                both = inner_dot(stacked, bands[0])
                products.append(both[:2 * piece] + both[2 * piece:] + inner_dot(high, bands[1]))
            real = products[0][:piece] - products[1][piece:]
            imag = products[0][piece:] + products[1][:piece]
            for member in range(members):
                target = tile_index * members + member
                self.back_chunks[field, target, :piece, :] = real[:, member * rows:(member + 1) * rows]
                self.back_chunks[field, target, piece:, :] = imag[:, member * rows:(member + 1) * rows]
            for step in range(members):
                hop = turn * members + step
                if hop:
                    target = tile_index * members + (self.space + step) % members
                    self.back_in[field].append(self.push(
                        self.back_chunks.at[field, target], self.gathered.at[field, self.vel, self.space],
                        self.back_send.at[field, hop], self.back_recv.at[field, hop], {"space": target},
                    ))
        self.gathered[field, self.vel, self.space] = self.back_chunks[field, self.space]

    def spread_stage(self, field):
        arrivals, core_copies = [], []
        for hop in range(self.spaces):
            source = self.back_source(hop)
            if hop:
                self.back_in[field][hop].wait_recv()
            chunk = self.gathered.at[field, self.vel, source]
            for far in range(1, self.groups // 2):
                arrivals.append((far, hop, self.push(
                    chunk, chunk, self.far_send.at[field, far, hop], self.far_recv.at[field, far, hop],
                    {"vel": self.far_peer(far)},
                )))
            core_copies.append(self.push(
                chunk, chunk, self.core_send.at[field, 0, hop], self.core_recv.at[field, 0, hop],
                {"vel": self.core_peer},
            ))
        for far, hop, copy in arrivals:
            copy.wait_recv()
            source = self.back_source(hop)
            origin = self.far_peer(self.groups // 2 - far)
            chunk = self.gathered.at[field, origin, source]
            core_copies.append(self.push(
                chunk, chunk, self.core_send.at[field, far, hop], self.core_recv.at[field, far, hop],
                {"vel": self.core_peer},
            ))
        for copy in core_copies:
            copy.wait_recv()

    def finish(self, field, out_ref):
        piece = self.piece
        for start in range(0, self.width, BAND):
            group = start // self.columns
            first = (start % self.columns) // piece
            for part in range(2):
                block = jnp.concatenate([
                    self.gathered[field, group, source, part * piece:(part + 1) * piece, :]
                    for source in range(first, first + BAND // piece)
                ], axis=0)
                out_ref[part, :, start:start + BAND] = block.T

    def leave(self):
        for copy in self.sent:
            copy.wait_send()


def first_kernel(spaces, groups, probe_ref, control_ref, table_ref, probe_out, control_out, *scratch):
    _, rows, width = probe_ref.shape
    mixer = Mixer(spaces, groups, width, rows, table_ref, scratch)
    mixer.enter()
    mixer.columns_stage(0, mixer.columns_mix(mixer.vel, probe_ref[0], probe_ref[1]))
    mixer.columns_stage(1, mixer.columns_mix(mixer.vel, control_ref[0], control_ref[1]))
    mixer.rows_stage(0)
    mixer.rows_stage(1)
    mixer.spread_stage(0)
    mixer.finish(0, probe_out)
    mixer.spread_stage(1)
    mixer.finish(1, control_out)
    mixer.leave()


def second_kernel(spaces, groups, probe_ref, control_ref, part_ref, table_ref, chunks_out,
                  core_part, own_mix, far_mix, far_in, sum_send, sum_recv, out_sems, *scratch):
    _, rows, width = probe_ref.shape
    mixer = Mixer(spaces, groups, width, rows, table_ref, scratch)
    mixer.enter()
    swap = mixer.push(part_ref, core_part, sum_send.at[0], sum_recv.at[0], {"vel": mixer.core_peer})
    mixer.columns_stage(0, mixer.columns_mix(mixer.vel, control_ref[0], control_ref[1]))
    swap.wait_recv()
    core_part[...] = COUPLE * (core_part[...] + part_ref[...])
    swaps = []
    for far in range(1, groups // 2):
        real, imag = mixer.columns_mix(mixer.far_peer(far), -core_part[1], core_part[0])
        far_mix[far, 0] = real
        far_mix[far, 1] = imag
        swaps.append(mixer.push(
            far_mix.at[far], far_in.at[far], sum_send.at[far], sum_recv.at[far], {"vel": mixer.far_peer(far)},
        ))
    real, imag = mixer.columns_mix(mixer.vel, probe_ref[0] - core_part[1], probe_ref[1] + core_part[0])
    own_mix[0] = real
    own_mix[1] = imag
    mixer.rows_stage(0)
    whole = [own_mix[0], own_mix[1]]
    for far, copy in enumerate(swaps, 1):
        copy.wait_recv()
        whole = [whole[0] + far_in[far, 0], whole[1] + far_in[far, 1]]
    mixer.columns_stage(1, whole)
    mixer.spread_stage(0)
    control_copy = pltpu.make_async_copy(mixer.gathered.at[0], chunks_out.at[0], out_sems.at[0])
    control_copy.start()
    mixer.rows_stage(1)
    mixer.spread_stage(1)
    probe_copy = pltpu.make_async_copy(mixer.gathered.at[1], chunks_out.at[1], out_sems.at[1])
    probe_copy.start()
    mixer.leave()
    control_copy.wait()
    probe_copy.wait()


def assemble_kernel(chunks_ref, control_out, probe_out):
    _, _, spaces, tall, _ = chunks_ref.shape
    piece = tall // 2
    for field, out_ref in enumerate((control_out, probe_out)):
        for start in range(0, spaces * piece, BAND):
            for part in range(2):
                block = jnp.concatenate([
                    chunks_ref[field, 0, source, part * piece:(part + 1) * piece, :]
                    for source in range(start // piece, (start + BAND) // piece)
                ], axis=0)
                out_ref[part, :, start:start + BAND] = block.T


def assemble(chunks):
    _, groups, spaces, tall, rows = chunks.shape
    columns = spaces * tall // 2
    shape = jax.ShapeDtypeStruct((2, rows, groups * columns), jnp.float32)
    out = pl.BlockSpec((2, rows, columns), lambda i: (0, 0, i))
    return pl.pallas_call(
        assemble_kernel,
        grid=(groups,),
        in_specs=[pl.BlockSpec((2, 1, spaces, tall, rows), lambda i: (0, i, 0, 0, 0))],
        out_specs=[out, out],
        out_shape=[shape, shape],
        compiler_params=pltpu.CompilerParams(vmem_limit_bytes=60 * 1024 * 1024),
        name="assemble_fields",
    )(chunks)


def diffract(kernel, spaces, groups, collective, fields, extra, table):
    _, rows, width = fields[0].shape
    piece = width // groups // spaces
    chunks = pltpu.VMEM((2, spaces, 2 * piece, rows), jnp.float32)
    dma = pltpu.SemaphoreType.DMA
    scratch = [
        pltpu.VMEM((2 * rows, width), jnp.bfloat16),
        pltpu.VMEM((2 * rows, width), jnp.bfloat16),
        chunks, chunks, chunks,
        pltpu.VMEM((2, groups, spaces, 2 * piece, rows), jnp.float32),
        dma((2, spaces)), dma((2, spaces)), dma((2, spaces)), dma((2, spaces)),
        dma((2, groups // 2, spaces)), dma((2, groups // 2, spaces)),
        dma((2, groups // 2, spaces)), dma((2, groups // 2, spaces)),
    ]
    shape = jax.ShapeDtypeStruct(fields[0].shape, jnp.float32)
    vmem = pl.BlockSpec(memory_space=pltpu.VMEM)
    out_shape, out_specs = [shape, shape], [vmem, vmem]
    if extra:
        mixes = pltpu.VMEM((groups // 2, 2, width // groups, rows), jnp.float32)
        scratch = [
            pltpu.VMEM((2, rows, width), jnp.float32),
            pltpu.VMEM((2, width // groups, rows), jnp.float32), mixes, mixes,
            dma((groups // 2,)), dma((groups // 2,)), dma((2,)),
        ] + scratch
        out_shape = jax.ShapeDtypeStruct((2, groups, spaces, 2 * piece, rows), jnp.float32)
        out_specs = pl.BlockSpec(memory_space=pl.ANY)
    operands = (*fields, *extra, table)
    return pl.pallas_call(
        functools.partial(kernel, spaces, groups),
        in_specs=[vmem] * len(operands),
        out_specs=out_specs,
        out_shape=out_shape,
        scratch_shapes=scratch,
        compiler_params=pltpu.CompilerParams(collective_id=collective, has_side_effects=True, vmem_limit_bytes=60 * 1024 * 1024),
        name=kernel.__name__,
    )(*operands)


def state_kernel(doppler_ref, weight_ref, probe_ref, control_ref, gradient_ref, optical_ref, spin_ref, optical_out, spin_out, total_ref, *, scale):
    classes = optical_ref.shape[1]
    width = optical_ref.shape[3]
    step = DT
    half = 0.5 * DT * DT

    def lane_block(block, carry):
        lanes = pl.ds(pl.multiple_of(block * 128, 128), 128)
        probe_real, probe_imag = probe_ref[0, :, lanes], probe_ref[1, :, lanes]
        control_real, control_imag = control_ref[0, :, lanes], control_ref[1, :, lanes]
        gradient = gradient_ref[:, lanes]
        power = half * (control_real * control_real + control_imag * control_imag)
        keep_real = step - half * (GAMMA + DEPHASE)
        keep_imag = -half * gradient
        into_real = -control_imag * keep_real - control_real * keep_imag
        into_imag = control_real * keep_real - control_imag * keep_imag
        back_real = control_imag * keep_real - control_real * keep_imag
        back_imag = control_real * keep_real + control_imag * keep_imag
        slope_real, slope_imag = half * control_real, half * control_imag
        source_real = -(step - half * GAMMA) * probe_imag
        source_imag = (step - half * GAMMA) * probe_real
        drive_real, drive_imag = half * probe_real, half * probe_imag
        spin_source_real = -half * (control_real * probe_real + control_imag * probe_imag)
        spin_source_imag = -half * (control_real * probe_imag - control_imag * probe_real)
        decay_real = 1.0 - step * DEPHASE + half * (DEPHASE * DEPHASE - gradient * gradient) - power
        decay_imag = (2.0 * half * DEPHASE - step) * gradient
        sum_real = jnp.zeros_like(gradient)
        sum_imag = jnp.zeros_like(gradient)
        for item in range(classes):
            shift = doppler_ref[item]
            weight = weight_ref[item] * scale
            self_real = (1.0 - step * GAMMA + half * (GAMMA * GAMMA - shift * shift)) - power
            self_imag = (2.0 * half * GAMMA - step) * shift
            turn_real, turn_imag = shift * slope_real, shift * slope_imag
            pull_real, pull_imag = into_real + turn_real, into_imag + turn_imag
            push_real, push_imag = back_real + turn_real, back_imag - turn_imag
            a_real, a_imag = optical_ref[0, item, :, lanes], optical_ref[1, item, :, lanes]
            b_real, b_imag = spin_ref[0, item, :, lanes], spin_ref[1, item, :, lanes]
            new_real = (
                self_real * a_real - self_imag * a_imag + pull_real * b_real - pull_imag * b_imag
                + (source_real + shift * drive_real)
            )
            new_imag = (
                self_real * a_imag + self_imag * a_real + pull_real * b_imag + pull_imag * b_real
                + (source_imag + shift * drive_imag)
            )
            optical_out[0, item, :, lanes] = new_real
            optical_out[1, item, :, lanes] = new_imag
            spin_out[0, item, :, lanes] = (
                push_real * a_real - push_imag * a_imag + decay_real * b_real - decay_imag * b_imag + spin_source_real
            )
            spin_out[1, item, :, lanes] = (
                push_real * a_imag + push_imag * a_real + decay_real * b_imag + decay_imag * b_real + spin_source_imag
            )
            sum_real += weight * new_real
            sum_imag += weight * new_imag
        total_ref[0, :, lanes] = sum_real
        total_ref[1, :, lanes] = sum_imag
        return carry

    lax.fori_loop(0, width // 128, lane_block, 0)


def advance(optical, spin_part, probe_part, control, doppler, weight, gradient, scale):
    _, classes, rows, width = optical.shape
    tall = min(16, rows)
    state = pl.BlockSpec((2, classes, tall, width), lambda i: (0, 0, i, 0))
    plane = pl.BlockSpec((2, tall, width), lambda i: (0, i, 0))
    small = pl.BlockSpec(memory_space=pltpu.SMEM)
    return pl.pallas_call(
        functools.partial(state_kernel, scale=scale),
        grid=(rows // tall,),
        in_specs=[small, small, plane, plane, pl.BlockSpec((tall, width), lambda i: (i, 0)), state, state],
        out_specs=[state, state, plane],
        out_shape=[
            jax.ShapeDtypeStruct(optical.shape, jnp.float32),
            jax.ShapeDtypeStruct(spin_part.shape, jnp.float32),
            jax.ShapeDtypeStruct((2, rows, width), jnp.float32),
        ],
        compiler_params=pltpu.CompilerParams(vmem_limit_bytes=60 * 1024 * 1024),
        name="advance_states",
    )(doppler, weight, probe_part, control, gradient, optical, spin_part)


def shards(
    spaces,
    groups,
    probe_field,
    control_field,
    optical_state,
    spin_state,
    doppler_shift,
    class_weight,
    gradient_shift,
):
    table = mixing_tables(probe_field.shape[2])
    probe_one, control_one = diffract(first_kernel, spaces, groups, 0, (probe_field, control_field), (), table)
    optical_new, spin_new, weighted = advance(
        optical_state,
        spin_state,
        probe_one,
        control_one,
        doppler_shift,
        class_weight,
        gradient_shift,
        1.0 / (optical_state.shape[1] * groups),
    )
    control_out, probe_out = assemble(diffract(second_kernel, spaces, groups, 1, (probe_one, control_one), (weighted,), table))
    return (probe_out, control_out, optical_new, spin_new)


def solution(mesh):
    return jax.shard_map(
        functools.partial(shards, mesh.shape["space"], mesh.shape["vel"]),
        mesh=mesh,
        in_specs=(
            P(None, "space", None),
            P(None, "space", None),
            P(None, "vel", "space", None),
            P(None, "vel", "space", None),
            P("vel"),
            P("vel"),
            P("space", None),
        ),
        out_specs=(
            P(None, "space", None),
            P(None, "space", None),
            P(None, "vel", "space", None),
            P(None, "vel", "space", None),
        ),
        check_vma=False,
    )
```
